32 devices in a mesh: row: 16 (over z, y, core), col: 2 (over x).
Axes of the slice: x: 2, y: 2, z: 4, core: 2. Of those that a mesh axis runs over, the one named last changes fastest.
Arguments:
- latents: bfloat16 [16, 1152, 1024], P('row', 'col'), may hold values from -6 to 6
- labels: int32 [16], replicated, may hold values from 0 to 1000
- timesteps: int32 [16], replicated, may hold values from 0 to 999
- label_table: bfloat16 [1152, 1001], P('col'), may hold values from -6 to 6
- ada_weight: bfloat16 [6, 1152, 1152], P(None, 'col'), may hold values from -0.1875 to 0.1875
- ada_bias: bfloat16 [6, 1152], P(None, 'col'), may hold values from -3 to 3
- qkv_weight: bfloat16 [1152, 3, 1152], P('row', None, 'col'), may hold values from -0.1875 to 0.1875
- qv_bias: bfloat16 [2, 1152], P(None, 'col'), may hold values from -3 to 3
- proj_weight: bfloat16 [1152, 1152], P('col', 'row'), may hold values from -2 to 2
- proj_bias: bfloat16 [1152], P('col'), may hold values from -3 to 3
- expand_weight: bfloat16 [1152, 4608], P('row', 'col'), may hold values from -0.1875 to 0.1875
- expand_bias: bfloat16 [4608], P('col'), may hold values from -3 to 3
- contract_weight: bfloat16 [4608, 1152], P('col', 'row'), may hold values from -0.09375 to 0.09375
- contract_bias: bfloat16 [1152], P('col'), may hold values from -3 to 3
- cotangent: bfloat16 [16, 1152, 1024], P('row', 'col'), may hold values from -6 to 6
Outputs:
- block_out: float32 [16, 1152, 1024], P('row', 'col')
- grad_latents: float32 [16, 1152, 1024], P('row', 'col')
- grad_qkv: float32 [1152, 3, 1152], P('row', None, 'col')
- grad_qv_bias: float32 [2, 1152], P(None, 'col')
- grad_proj: float32 [1152, 1152], P('col', 'row')
- grad_proj_bias: float32 [1152], P('col')
- grad_expand: float32 [1152, 4608], P('row', 'col')
- grad_expand_bias: float32 [4608], P('col')
- grad_contract: float32 [4608, 1152], P('col', 'row')
- grad_contract_bias: float32 [1152], P('col')
- grad_ada: float32 [6, 1152, 1152], P(None, 'col')
- grad_ada_bias: float32 [6, 1152], P(None, 'col')
- grad_cond: float32 [16, 1152], P('row', 'col')
- grad_table: float32 [1152, 1001], P('col')
The draws below stay inside these ranges and needn't reach their ends.
All inputs are finite; a program needn't handle non-finite values.
Results may differ from the reference program's by a relative error of at most 0.023.
Values may be sent and summed in bfloat16 or wider, within the bound.
No kernel may reach another device: no remote copies, remote signals or barrier semaphores. Data moves between devices by JAX's collectives and lax.ppermute only.
A program may use at most 256 MiB of HBM per device.

```python
import math
import jax
import jax.numpy as jnp
from jax import lax

D = 1152
HEADS = 16
HEAD = 72
FF = 4608
CLASSES = 1001
LEN = 1024
SEQS = 16


def place_ends(array, rng, smallest, top_value):
    longest = array.shape.index(max(array.shape))
    spots = []
    for shift in (0, 1):
        where = [jax.random.randint(jax.random.fold_in(rng, axis), (), 0, length) for axis, length in enumerate(array.shape)]
        where[longest] = (where[longest] + shift) % array.shape[longest]
        spots.append(tuple(where))
    return array.at[spots[0]].set(smallest).at[spots[1]].set(top_value)


def level_of(stream_key, extent, shards, least, top_value):
    def one(position, blocks):
        draws = jax.random.uniform(jax.random.fold_in(jax.random.fold_in(stream_key, 6), position), (blocks,), jnp.float32, least / len(shards), top_value / len(shards))
        return jnp.repeat(jnp.exp(draws), extent[position] // blocks).reshape((-1,) + (1,) * (len(extent) - position - 1))

    gain = one(*shards[0])
    for cut in shards[1:]:
        gain = gain * one(*cut)
    return gain


def scatter_about(own_key, dims, deviation, reach, pieces=(), kind=jnp.bfloat16):
    drawn = deviation * jax.random.normal(own_key, dims, jnp.float32)
    if pieces:
        drawn = drawn * level_of(own_key, dims, pieces, -0.22, 0.18)
    return jnp.clip(drawn, -reach, reach).astype(kind)


def setup_inputs(seed: int = 0) -> dict:
    key_of = jax.random.split(jax.random.key(seed), 16)
    return {
        "latents": scatter_about(key_of[0], (SEQS, D, LEN), 1.0, 6.0, ((0, 16), (1, 2))),
        "labels": place_ends(jax.random.randint(key_of[1], (SEQS,), 0, CLASSES), jax.random.fold_in(key_of[1], 1), 0, CLASSES - 1).astype(jnp.int32),
        "timesteps": place_ends(jax.random.randint(key_of[2], (SEQS,), 0, 1000), jax.random.fold_in(key_of[2], 1), 0, 999).astype(jnp.int32),
        "label_table": scatter_about(key_of[3], (D, CLASSES), 1.0, 6.0, ((0, 2),)),
        "ada_weight": scatter_about(key_of[4], (6, D, D), D ** -0.5, 0.1875, ((1, 2),)),
        "ada_bias": scatter_about(key_of[5], (6, D), 0.5, 3.0, ((1, 2),)),
        "qkv_weight": scatter_about(key_of[6], (D, 3, D), D ** -0.5, 0.1875, ((0, 16), (2, 2))),
        "qv_bias": scatter_about(key_of[7], (2, D), 0.5, 3.0, ((1, 2),)),
        "proj_weight": scatter_about(key_of[8], (D, D), (max(D // 128, 1)) ** -0.5, 2.0, ((0, 2), (1, 16))),
        "proj_bias": scatter_about(key_of[9], (D,), 0.5, 3.0, ((0, 2),)),
        "expand_weight": scatter_about(key_of[10], (D, FF), D ** -0.5, 0.1875, ((0, 16), (1, 2))),
        "expand_bias": scatter_about(key_of[11], (FF,), 0.5, 3.0, ((0, 2),)),
        "contract_weight": scatter_about(key_of[12], (FF, D), FF ** -0.5, 0.09375, ((0, 2), (1, 16))),
        "contract_bias": scatter_about(key_of[13], (D,), 0.5, 3.0, ((0, 2),)),
        "cotangent": scatter_about(key_of[14], (SEQS, D, LEN), 1.0, 6.0, ((0, 16), (1, 2))),
    }


EPSILON = 1e-06
GELU_COEF = 0.7978845608028654

def gelu_tanh(values):
    return 0.5 * values * (1.0 + jnp.tanh(GELU_COEF * (values + 0.044715 * values * values * values)))

def sinusoid(timesteps, feature, full_width):
    half_width = full_width // 2
    frequency = jnp.exp(-math.log(10000.0) * (feature % half_width).astype(jnp.float32) / half_width)
    angles = timesteps.astype(jnp.float32)[:, None] * frequency[None, :]
    return jnp.where(feature[None, :] < half_width, jnp.cos(angles), jnp.sin(angles))

def layer_norm(values):
    average = lax.optimization_barrier(jnp.mean(values, axis=-1, keepdims=True))
    spread = lax.optimization_barrier(jnp.mean(values * values, axis=-1, keepdims=True)) - average * average
    inverse = lax.rsqrt(spread + EPSILON)
    return ((values - average) * inverse, inverse)

def norm_back(grad_normed, normed, inverse):
    first_mean = lax.optimization_barrier(jnp.mean(grad_normed, axis=-1, keepdims=True))
    cross_mean = lax.optimization_barrier(jnp.mean(grad_normed * normed, axis=-1, keepdims=True))
    return inverse * (grad_normed - first_mean - normed * cross_mean)

def matmul(left_side, right_side):
    return jnp.dot(left_side, right_side, preferred_element_type=jnp.float32)

def as_heads(values):
    return values.astype(jnp.float32).reshape(values.shape[0], HEADS, HEAD)

def rounded(values):
    return lax.optimization_barrier(values.astype(jnp.bfloat16)).astype(jnp.float32)

def reference(latents, labels, timesteps, label_table, ada_weight, ada_bias, qkv_weight, qv_bias, proj_weight, proj_bias, expand_weight, expand_bias, contract_weight, contract_bias, cotangent):
    score_scale = 1.0 / math.sqrt(HEAD)
    feature = jnp.arange(D, dtype=jnp.int32)
    cond = label_table.T[labels].astype(jnp.float32) + sinusoid(timesteps, feature, D)
    silu_cond = jax.nn.silu(cond).astype(jnp.bfloat16)
    ada_flat = ada_weight.transpose(2, 0, 1).reshape(D, 6 * D)
    modulation = (matmul(silu_cond, ada_flat) + ada_bias.reshape(6 * D).astype(jnp.float32)).reshape(SEQS, 6, D)
    triple_weight = qkv_weight.reshape(D, 3 * D)
    token_latents = latents.transpose(0, 2, 1)
    token_tangent = cotangent.transpose(0, 2, 1)

    def one_sequence(totals, inputs):
        tokens, offsets, tangent = inputs
        shift_first, scale_first, gate_first, shift_second, scale_second, gate_second = offsets
        start = tokens.astype(jnp.float32)
        normed_first, inv_first = layer_norm(start)
        in_first = (normed_first * (1.0 + scale_first) + shift_first).astype(jnp.bfloat16)
        triple = matmul(in_first, triple_weight).reshape(LEN, 3, D)
        query_rows = (triple[:, 0] + qv_bias[0]).astype(jnp.bfloat16)
        key_rows = triple[:, 1].astype(jnp.bfloat16)
        value_rows = (triple[:, 2] + qv_bias[1]).astype(jnp.bfloat16)
        query_heads = as_heads(query_rows)
        key_heads = as_heads(key_rows)
        value_heads = as_heads(value_rows)
        scores = jnp.einsum('qhd,khd->hqk', query_heads, key_heads) * score_scale
        row_top = lax.optimization_barrier(jnp.max(scores, axis=-1, keepdims=True))
        log_total = jnp.log(lax.optimization_barrier(jnp.sum(jnp.exp(scores - row_top), axis=-1, keepdims=True))) + row_top
        soft = jnp.exp(scores - log_total)
        soft_b = rounded(soft)
        attended = jnp.einsum('hqk,khd->qhd', soft_b, value_heads).reshape(LEN, D).astype(jnp.bfloat16)
        proj_out = matmul(attended, proj_weight) + proj_bias
        residual = start + gate_first * proj_out
        normed_second, inv_second = layer_norm(residual)
        in_second = (normed_second * (1.0 + scale_second) + shift_second).astype(jnp.bfloat16)
        pre_act = matmul(in_second, expand_weight) + expand_bias
        hidden = gelu_tanh(pre_act).astype(jnp.bfloat16)
        mlp_out = matmul(hidden, contract_weight) + contract_bias
        block_out = residual + gate_second * mlp_out
        grad_out = tangent.astype(jnp.float32)
        grad_mlp = grad_out * gate_second
        grad_mlp_b = grad_mlp.astype(jnp.bfloat16)
        contract_term = matmul(hidden.T, grad_mlp_b)
        grad_hidden = matmul(grad_mlp_b, contract_weight.T)
        grad_pre = jax.vjp(gelu_tanh, pre_act)[1](grad_hidden)[0]
        grad_pre_b = grad_pre.astype(jnp.bfloat16)
        expand_term = matmul(in_second.T, grad_pre_b)
        grad_in_second = matmul(grad_pre_b, expand_weight.T)
        grad_residual = grad_out + norm_back(grad_in_second * (1.0 + scale_second), normed_second, inv_second)
        grad_proj_out = grad_residual * gate_first
        grad_proj_b = grad_proj_out.astype(jnp.bfloat16)
        proj_term = matmul(attended.T, grad_proj_b)
        grad_att = matmul(grad_proj_b, proj_weight.T).astype(jnp.bfloat16)
        grad_att_heads = as_heads(grad_att)
        grad_value_heads = jnp.einsum('hqk,qhd->khd', soft_b, grad_att_heads)
        grad_soft = jnp.einsum('qhd,khd->hqk', grad_att_heads, value_heads)
        row_delta = jnp.einsum('qhd,qhd->hq', grad_att_heads, as_heads(attended))[:, :, None]
        grad_scores = rounded(soft * (grad_soft - row_delta))
        grad_query = jnp.einsum('hqk,khd->qhd', grad_scores, key_heads).reshape(LEN, D) * score_scale
        grad_keys = jnp.einsum('hqk,qhd->khd', grad_scores, query_heads).reshape(LEN, D) * score_scale
        grad_values = grad_value_heads.reshape(LEN, D)
        grad_triple = jnp.stack((grad_query, grad_keys, grad_values), axis=1).astype(jnp.bfloat16).reshape(LEN, 3 * D)
        triple_term = matmul(in_first.T, grad_triple)
        grad_in_first = matmul(grad_triple, triple_weight.T)
        grad_latents = grad_residual + norm_back(grad_in_first * (1.0 + scale_first), normed_first, inv_first)
        grad_offsets = jnp.stack((lax.optimization_barrier(jnp.sum(grad_in_first, axis=0)), lax.optimization_barrier(jnp.sum(grad_in_first * normed_first, axis=0)), lax.optimization_barrier(jnp.sum(grad_residual * proj_out, axis=0)), lax.optimization_barrier(jnp.sum(grad_in_second, axis=0)), lax.optimization_barrier(jnp.sum(grad_in_second * normed_second, axis=0)), lax.optimization_barrier(jnp.sum(grad_out * mlp_out, axis=0))))
        terms = (triple_term, jnp.stack((lax.optimization_barrier(jnp.sum(grad_query, axis=0)), lax.optimization_barrier(jnp.sum(grad_values, axis=0)))), proj_term, lax.optimization_barrier(jnp.sum(grad_proj_out, axis=0)), expand_term, lax.optimization_barrier(jnp.sum(grad_pre, axis=0)), contract_term, lax.optimization_barrier(jnp.sum(grad_mlp, axis=0)))
        new_totals = jax.tree.map(lambda total, term: total + term, totals, terms)
        return (new_totals, (block_out, grad_latents, grad_offsets))
    zero_totals = (jnp.zeros((D, 3 * D), jnp.float32), jnp.zeros((2, D), jnp.float32), jnp.zeros((D, D), jnp.float32), jnp.zeros((D,), jnp.float32), jnp.zeros((D, FF), jnp.float32), jnp.zeros((FF,), jnp.float32), jnp.zeros((FF, D), jnp.float32), jnp.zeros((D,), jnp.float32))
    totals, stacked = lax.scan(one_sequence, zero_totals, (token_latents, modulation, token_tangent))
    block_out, grad_latents, grad_mod = stacked
    triple_total, grad_qv_bias, grad_proj, grad_proj_bias, grad_expand, grad_expand_bias, grad_contract, grad_contract_bias = totals
    grad_ada_bias = lax.optimization_barrier(jnp.sum(grad_mod, axis=0))
    flat_grad = grad_mod.reshape(SEQS, 6 * D)
    grad_ada = jnp.dot(silu_cond.astype(jnp.float32).T, flat_grad, precision=lax.Precision.HIGHEST).reshape(D, 6, D).transpose(1, 2, 0)
    grad_silu = jnp.dot(flat_grad, ada_flat.astype(jnp.float32).T, precision=lax.Precision.HIGHEST)
    grad_cond = jax.vjp(jax.nn.silu, cond)[1](grad_silu)[0]
    label_hits = (labels[:, None] == jnp.arange(CLASSES, dtype=jnp.int32)[None, :]).astype(jnp.float32)
    grad_table = jnp.dot(grad_cond.T, label_hits, precision=lax.Precision.HIGHEST)
    return (block_out.transpose(0, 2, 1), grad_latents.transpose(0, 2, 1), triple_total.reshape(D, 3, D), grad_qv_bias, grad_proj, grad_proj_bias, grad_expand, grad_expand_bias, grad_contract, grad_contract_bias, grad_ada, grad_ada_bias, grad_cond, grad_table)
```

```python
import math

import jax
import jax.numpy as jnp
from jax import lax
from jax.sharding import PartitionSpec as P

D = 1152
HEAD = 72
CLASSES = 1001
EPSILON = 1e-06
GELU_COEF = 0.7978845608028654
AXES = ("row", "col")
F32 = jnp.float32
BF16 = jnp.bfloat16
HIGH = lax.Precision.HIGHEST


def gelu_tanh(values):
    return (
        0.5 * values * (1.0 + jnp.tanh(GELU_COEF * (values + 0.044715 * values * values * values)))
    )


def mm(left, right):
    return lax.dot_general(left, right, (((1,), (0,)), ((), ())), preferred_element_type=F32)


def mm_tn(left, right):
    return lax.dot_general(left, right, (((0,), (0,)), ((), ())), preferred_element_type=F32)


def mm_nt(left, right):
    return lax.dot_general(left, right, (((1,), (1,)), ((), ())), preferred_element_type=F32)


class Links:
    def __init__(self, rows, cols):
        self.count = rows * cols
        self.col_bits = cols.bit_length() - 1
        self.row_bits = rows.bit_length() - 1
        self.flat = lax.axis_index("row") * cols + lax.axis_index("col")
        self.x = 0
        self.ch = list(range(1, self.col_bits))
        self.core = self.col_bits
        self.rh = list(range(self.core + 1, self.core + self.row_bits))[::-1]
        self.order = {
            "a": self.rh + [self.x],
            "b": self.rh[:-1] + [self.x] + self.rh[-1:],
        }

    def bit(self, which):
        return (self.flat >> which) & 1

    def exchange(self, values, which):
        pairs = [(i, i ^ (1 << which)) for i in range(self.count)]
        return lax.ppermute(values, AXES, pairs)

    def swap(self, values):
        low, high = 1, 1 << self.core
        pairs = []
        for i in range(self.count):
            kept = i & ~(low | high)
            pairs.append((i, kept | (high if i & low else 0) | (low if i & high else 0)))
        return lax.ppermute(values, AXES, pairs)

    def joined(self, mine, theirs, which):
        low = self.bit(which) == 0
        return jnp.where(low, jnp.stack([mine, theirs]), jnp.stack([theirs, mine]))

    def gather(self, values, order):
        for which in order:
            values = self.joined(values, self.exchange(values, which), which)
        return values

    def gather_rows(self, values, stream):
        order = self.order[stream]
        natural = self.rh + [self.x]
        got = self.gather(values, order)
        have = order[::-1]
        tail = list(range(len(have), got.ndim))
        got = got.transpose([have.index(w) for w in natural] + tail)
        return got.reshape((-1,) + values.shape[1:])

    def scatter_rows(self, values, stream, rows):
        natural = self.rh + [self.x]
        sums = values.reshape((2,) * len(natural) + (values.shape[0] // rows,) + values.shape[1:])
        for which in self.order[stream][::-1]:
            axis = natural.index(which)
            natural = natural[:axis] + natural[axis + 1 :]
            own = self.bit(which)
            sent = lax.dynamic_index_in_dim(sums, 1 - own, axis, keepdims=False)
            kept = lax.dynamic_index_in_dim(sums, own, axis, keepdims=False)
            sums = kept + self.exchange(sent, which)
        return sums

    def gather_pair(self, values):
        got = self.gather(values, [self.core] + self.ch)
        return got.reshape((-1,) + values.shape[1:])

    def sum_pair(self, values):
        for which in [self.core] + self.ch:
            values = values + self.exchange(values.astype(BF16), which).astype(F32)
        return values


def norm_forward(values):
    average = jnp.mean(values, axis=0, keepdims=True)
    spread = jnp.mean(values * values, axis=0, keepdims=True) - average * average
    inverse = lax.rsqrt(spread + EPSILON)
    return (values - average) * inverse, inverse


def norm_backward(grad_normed, normed, inverse):
    first = jnp.mean(grad_normed, axis=0, keepdims=True)
    cross = jnp.mean(grad_normed * normed, axis=0, keepdims=True)
    return inverse * (grad_normed - first - normed * cross)


def heads_of(values):
    return values.reshape(values.shape[0] // HEAD, HEAD, values.shape[1])


def attend(query, key, value):
    scale = 1.0 / math.sqrt(HEAD)
    query, key, value = heads_of(query), heads_of(key), heads_of(value)
    scores = jnp.einsum("hdk,hdq->hkq", key, query, preferred_element_type=F32) * scale
    top = jnp.max(scores, axis=1, keepdims=True)
    log_total = jnp.log(jnp.sum(jnp.exp(scores - top), axis=1, keepdims=True)) + top
    soft_b = jnp.exp(scores - log_total).astype(BF16)
    out = jnp.einsum("hdk,hkq->hdq", value, soft_b, preferred_element_type=F32)
    return out.reshape(-1, out.shape[2]).astype(BF16), log_total


def attend_back(query, key, value, log_total, attended, grad_att):
    scale = 1.0 / math.sqrt(HEAD)
    query, key, value = heads_of(query), heads_of(key), heads_of(value)
    attended, grad_att = heads_of(attended), heads_of(grad_att)
    scores = jnp.einsum("hdk,hdq->hkq", key, query, preferred_element_type=F32) * scale
    soft = jnp.exp(scores - log_total)
    soft_b = soft.astype(BF16)
    grad_value = jnp.einsum("hkq,hdq->hdk", soft_b, grad_att, preferred_element_type=F32)
    grad_soft = jnp.einsum("hdk,hdq->hkq", value, grad_att, preferred_element_type=F32)
    delta = jnp.sum(grad_att.astype(F32) * attended.astype(F32), axis=1, keepdims=True)
    grad_scores = (soft * (grad_soft - delta)).astype(BF16)
    grad_query = jnp.einsum("hdk,hkq->hdq", key, grad_scores, preferred_element_type=F32) * scale
    grad_key = jnp.einsum("hdq,hkq->hdk", query, grad_scores, preferred_element_type=F32) * scale
    flat = lambda v: v.reshape(-1, v.shape[2])
    return flat(grad_query), flat(grad_key), flat(grad_value)


def make_on_device(rows, cols):
    def on_device(
        latents,
        labels,
        timesteps,
        label_table,
        ada_weight,
        ada_bias,
        qkv_weight,
        qv_bias,
        proj_weight,
        proj_bias,
        expand_weight,
        expand_bias,
        contract_weight,
        contract_bias,
        cotangent,
    ):
        links = Links(rows, cols)
        length = latents.shape[2]
        width = latents.shape[1]
        half = width // 2
        hidden_width = expand_weight.shape[1]
        hidden_half = hidden_width // 2
        seqs = labels.shape[0]
        chunk = qkv_weight.shape[0]
        row, col = lax.axis_index("row"), lax.axis_index("col")
        own_x, own_core = links.bit(links.x), links.bit(links.core)
        part = (col >> 1 << 1) + own_core

        qkv_own = links.swap(qkv_weight.reshape(chunk, 3 * width)).reshape(chunk, 3, width)
        streams = ("a", "b")
        qkv_w = [
            links.gather_rows(qkv_own[:, :, i * half : (i + 1) * half].reshape(chunk, 3 * half), s)
            for i, s in enumerate(streams)
        ]
        latents_own = links.swap(latents[0])
        latents_full = links.gather_pair(latents_own)
        proj_own = links.swap(proj_weight.T)
        proj_w = [
            links.gather_rows(proj_own[:, i * half : (i + 1) * half], s)
            for i, s in enumerate(streams)
        ]
        expand_own = links.swap(expand_weight)
        expand_w = [
            links.gather_rows(expand_own[:, i * hidden_half : (i + 1) * hidden_half], s)
            for i, s in enumerate(streams)
        ]
        contract_own = links.swap(contract_weight.T)
        contract_w = [
            links.gather_rows(contract_own[:, i * hidden_half : (i + 1) * hidden_half], s)
            for i, s in enumerate(streams)
        ]
        cotangent_full = links.gather_pair(links.swap(cotangent[0]))
        bias_rows = [
            qv_bias.astype(F32),
            proj_bias.astype(F32)[None],
            contract_bias.astype(F32)[None],
            expand_bias.astype(F32).reshape(-1, width),
        ]
        bias_own = links.swap(jnp.concatenate(bias_rows, axis=0))
        qv_own = bias_own[:2, :, None]
        pair_bias = links.gather([bias_own[2:4]][0], [links.core] + links.ch)
        pair_bias = pair_bias.reshape(-1, 2, width).transpose(1, 0, 2).reshape(2, D, 1)
        proj_b, contract_b = pair_bias[0], pair_bias[1]
        expand_b = bias_own[4:].reshape(hidden_width, 1)

        feature = col * width + jnp.arange(width, dtype=jnp.int32)
        half_width = D // 2
        frequency = jnp.exp(-math.log(10000.0) * (feature % half_width).astype(F32) / half_width)
        angles = timesteps.astype(F32)[:, None] * frequency[None, :]
        embedding = jnp.where(feature[None, :] < half_width, jnp.cos(angles), jnp.sin(angles))
        label_hits = labels[:, None] == jnp.arange(CLASSES, dtype=jnp.int32)[None, :]
        cond_part = mm_nt(label_hits.astype(BF16), label_table) + embedding
        cond_all = links.gather(cond_part, [links.x] + links.ch)
        cond_all = cond_all.reshape(-1, seqs, width).transpose(1, 0, 2).reshape(seqs, D)
        silu_all = jax.nn.silu(cond_all).astype(BF16)
        flat_ada = ada_weight.reshape(6 * width, D)
        pair = lax.dynamic_slice_in_dim(silu_all, (row >> 1) * 2, 2, 0)
        pair_mod = mm_nt(pair, flat_ada) + ada_bias.astype(F32).reshape(1, 6 * width)
        mine = lax.dynamic_index_in_dim(pair_mod, own_x, 0)
        other = lax.dynamic_index_in_dim(pair_mod, 1 - own_x, 0)
        mod = links.joined(mine, links.exchange(other, links.x), links.x)
        mod = links.gather(mod, links.ch)
        mod = mod.reshape(-1, 6, width).transpose(1, 0, 2).reshape(6, D, 1)
        shift_first, scale_first, gate_first, shift_second, scale_second, gate_second = [
            mod[i] for i in range(6)
        ]
        own_part = lambda v: lax.dynamic_slice_in_dim(v, part * width, width, 0)

        start = latents_full.astype(F32)
        normed_first, inv_first = norm_forward(start)
        in_first = (normed_first * (1.0 + scale_first) + shift_first).astype(BF16)
        heads = []
        for i in range(2):
            triple = mm_tn(qkv_w[i], in_first)
            qb, vb = [qv_own[j, i * half : (i + 1) * half] for j in range(2)]
            query = (triple[:half] + qb).astype(BF16)
            key = triple[half : 2 * half].astype(BF16)
            value = (triple[2 * half :] + vb).astype(BF16)
            heads.append((query, key, value) + attend(query, key, value))
        proj_out = (
            links.sum_pair(sum(mm(proj_w[i], heads[i][3]) for i in range(2))) + proj_b
        )
        residual = start + gate_first * proj_out
        normed_second, inv_second = norm_forward(residual)
        in_second = (normed_second * (1.0 + scale_second) + shift_second).astype(BF16)
        pre_act = [
            mm_tn(expand_w[i], in_second) + expand_b[i * hidden_half : (i + 1) * hidden_half]
            for i in range(2)
        ]
        hidden = [gelu_tanh(v).astype(BF16) for v in pre_act]
        mlp_out = links.sum_pair(sum(mm(contract_w[i], hidden[i]) for i in range(2))) + contract_b
        mlp_own = own_part(mlp_out)
        block_own = own_part(residual) + own_part(gate_second) * mlp_own
        block_out = links.swap(block_own.astype(BF16)).astype(F32)[None]

        grad_out = cotangent_full.astype(F32)
        grad_mlp_b = (grad_out * gate_second).astype(BF16)
        pre_grads = []
        grad_contract = []
        grad_expand = []
        for i in range(2):
            grad_contract.append(
                links.scatter_rows(mm_nt(grad_mlp_b, hidden[i]).astype(BF16), streams[i], rows)
            )
            grad_hidden = mm_tn(contract_w[i], grad_mlp_b)
            grad_pre = jax.vjp(gelu_tanh, pre_act[i])[1](grad_hidden)[0]
            pre_grads.append((grad_pre.astype(BF16), jnp.sum(grad_pre, axis=1)))
        for i in range(2):
            grad_expand.append(
                links.scatter_rows(mm_nt(in_second, pre_grads[i][0]).astype(BF16), streams[i], rows)
            )
        grad_in_second = links.sum_pair(sum(mm(expand_w[i], pre_grads[i][0]) for i in range(2)))
        grad_residual = grad_out + norm_backward(
            grad_in_second * (1.0 + scale_second), normed_second, inv_second
        )
        grad_proj_out = grad_residual * gate_first
        grad_proj_b = grad_proj_out.astype(BF16)
        grad_proj = []
        triple_grads = []
        qv_sums = []
        grad_qkv = []
        for i in range(2):
            query, key, value, attended, log_total = heads[i]
            grad_proj.append(
                links.scatter_rows(mm_nt(grad_proj_b, attended).astype(BF16), streams[i], rows)
            )
            grad_att = mm_tn(proj_w[i], grad_proj_b).astype(BF16)
            gq, gk, gv = attend_back(query, key, value, log_total, attended, grad_att)
            qv_sums.append((jnp.sum(gq, axis=1), jnp.sum(gv, axis=1)))
            triple_grads.append(jnp.concatenate([v.astype(BF16) for v in (gq, gk, gv)], axis=0))
            grad_qkv.append(
                links.scatter_rows(mm_nt(in_first, triple_grads[i]).astype(BF16), streams[i], rows)
            )
        grad_in_first = links.sum_pair(sum(mm(qkv_w[i], triple_grads[i]) for i in range(2)))
        grad_latents_full = grad_residual + norm_backward(
            grad_in_first * (1.0 + scale_first), normed_first, inv_first
        )
        grad_latents = links.swap(own_part(grad_latents_full).astype(BF16)).astype(F32)[None]

        token_sum = lambda v: jnp.sum(v, axis=1)[None]
        own_out = own_part(grad_out)
        own_in_second = own_part(grad_in_second)
        own_in_first = own_part(grad_in_first)
        early = jnp.concatenate(
            [
                token_sum(own_part(grad_residual) * own_part(proj_out)),
                token_sum(own_in_second),
                token_sum(own_in_second * own_part(normed_second)),
                token_sum(own_out * mlp_own),
                token_sum(own_part(grad_proj_out)),
                token_sum(own_out * own_part(gate_second)),
                jnp.concatenate([p[1] for p in pre_grads]).reshape(-1, width),
            ],
            axis=0,
        )
        late = jnp.concatenate(
            [
                token_sum(own_in_first),
                token_sum(own_in_first * own_part(normed_first)),
                jnp.concatenate([s[0] for s in qv_sums])[None],
                jnp.concatenate([s[1] for s in qv_sums])[None],
            ],
            axis=0,
        )
        wide = lambda v: links.swap(links.gather_rows(v[None], "a"))
        early_all, late_all = wide(early), wide(late)
        grad_mod = jnp.concatenate([late_all[:, :2], early_all[:, :4]], axis=1)
        sums = jnp.sum(early_all[:, 4:], axis=0)
        grad_qv_bias = jnp.sum(late_all[:, 2:4], axis=0)
        grad_proj_bias, grad_contract_bias = sums[0], sums[1]
        grad_expand_bias = sums[2:].reshape(hidden_width)
        grad_ada_bias = jnp.sum(grad_mod, axis=0)
        flat_grad = grad_mod.reshape(seqs, 6 * width)
        grad_ada = lax.dot_general(
            flat_grad, silu_all.astype(F32), (((0,), (0,)), ((), ())), precision=HIGH
        ).reshape(6, width, D)
        grad_silu = jnp.dot(flat_grad, flat_ada.astype(F32), precision=HIGH)
        for which in [links.x] + links.ch:
            grad_silu = grad_silu + links.exchange(grad_silu, which)
        grad_cond_all = jax.vjp(jax.nn.silu, cond_all)[1](grad_silu)[0]
        grad_cond_cols = lax.dynamic_slice_in_dim(grad_cond_all, col * width, width, 1)
        grad_cond = lax.dynamic_slice_in_dim(grad_cond_cols, row, 1, 0)
        grad_table = lax.dot_general(
            grad_cond_cols, label_hits.astype(F32), (((0,), (0,)), ((), ())), precision=HIGH
        )

        back = lambda v: links.swap(jnp.concatenate(v, axis=1)).astype(F32)
        qkv_parts = [v.reshape(chunk, 3, half) for v in grad_qkv]
        qkv_back = jnp.concatenate(qkv_parts, axis=2).reshape(chunk, 3 * width)
        grad_qkv = links.swap(qkv_back).astype(F32).reshape(chunk, 3, width)
        return (
            block_out,
            grad_latents,
            grad_qkv,
            grad_qv_bias,
            back(grad_proj).T,
            grad_proj_bias,
            back(grad_expand),
            grad_expand_bias,
            back(grad_contract).T,
            grad_contract_bias,
            grad_ada,
            grad_ada_bias,
            grad_cond,
            grad_table,
        )

    return on_device


def solution(mesh):
    in_specs = (
        P("row", "col", None),
        P(),
        P(),
        P("col", None),
        P(None, "col", None),
        P(None, "col"),
        P("row", None, "col"),
        P(None, "col"),
        P("col", "row"),
        P("col"),
        P("row", "col"),
        P("col"),
        P("col", "row"),
        P("col"),
        P("row", "col", None),
    )
    out_specs = (
        P("row", "col", None),
        P("row", "col", None),
        P("row", None, "col"),
        P(None, "col"),
        P("col", "row"),
        P("col"),
        P("row", "col"),
        P("col"),
        P("col", "row"),
        P("col"),
        P(None, "col", None),
        P(None, "col"),
        P("row", "col"),
        P("col", None),
    )
    return jax.shard_map(
        make_on_device(mesh.shape["row"], mesh.shape["col"]),
        mesh=mesh,
        in_specs=in_specs,
        out_specs=out_specs,
        check_vma=False,
    )
```

```python
import functools
import math

import jax
import jax.numpy as jnp
from jax import lax
from jax.experimental import pallas as pl
from jax.experimental.pallas import tpu as pltpu
from jax.sharding import PartitionSpec as P

D = 1152
HEAD = 72
CLASSES = 1001
EPSILON = 1e-06
GELU_COEF = 0.7978845608028654
AXES = ("rz", "ry", "rl", "ch", "cl")
ROW, COL = AXES[:3], AXES[3:]
GROUP = ("rz", "ry", "cl")
F32 = jnp.float32
BF16 = jnp.bfloat16
HIGH = lax.Precision.HIGHEST
LOG2E = math.log2(math.e)
BLOCK = 256
VMEM_LIMIT = 48 * 1024 * 1024


def gelu_tanh(values):
    return (
        0.5 * values * (1.0 + jnp.tanh(GELU_COEF * (values + 0.044715 * values * values * values)))
    )


def mm(left, right):
    return lax.dot_general(left, right, (((1,), (0,)), ((), ())), preferred_element_type=F32)


def mm_tn(left, right):
    return lax.dot_general(left, right, (((0,), (0,)), ((), ())), preferred_element_type=F32)


def mm_nt(left, right):
    return lax.dot_general(left, right, (((1,), (1,)), ((), ())), preferred_element_type=F32)


class Links:
    def __init__(self, rows, cols):
        self.count = rows * cols
        self.col_bits = cols.bit_length() - 1
        self.row_bits = rows.bit_length() - 1
        self.flat = lax.axis_index(AXES)
        self.x = 0
        self.ch = list(range(1, self.col_bits))
        self.core = self.col_bits
        self.rh = list(range(self.core + 1, self.core + self.row_bits))[::-1]
        self.order = {
            "a": self.rh + [self.x],
            "b": self.rh[:-1] + [self.x] + self.rh[-1:],
            "c": [self.x] + self.rh[::-1],
        }

    def bit(self, which):
        return (self.flat >> which) & 1

    def exchange(self, values, which):
        pairs = [(i, i ^ (1 << which)) for i in range(self.count)]
        return lax.ppermute(values, AXES, pairs)

    def swap(self, values):
        low, high = 1, 1 << self.core
        pairs = [
            (i, i ^ (low | high))
            for i in range(self.count)
            if bool(i & low) != bool(i & high)
        ]
        moved = lax.ppermute(values, AXES, pairs)
        return jnp.where(self.bit(self.x) == self.bit(self.core), values, moved)

    def joined(self, mine, theirs, which):
        low = self.bit(which) == 0
        return jnp.where(low, jnp.stack([mine, theirs]), jnp.stack([theirs, mine]))

    def gather(self, values, order):
        for which in order:
            values = self.joined(values, self.exchange(values, which), which)
        return values

    def gather_rows(self, values, stream):
        order = self.order[stream]
        natural = self.rh + [self.x]
        got = self.gather(values, order)
        have = order[::-1]
        tail = list(range(len(have), got.ndim))
        got = got.transpose([have.index(w) for w in natural] + tail)
        return got.reshape((-1,) + values.shape[1:])

    def scatter_rows(self, values, stream, rows):
        natural = self.rh + [self.x]
        sums = values.reshape((2,) * len(natural) + (values.shape[0] // rows,) + values.shape[1:])
        for which in self.order[stream][::-1]:
            axis = natural.index(which)
            natural = natural[:axis] + natural[axis + 1 :]
            own = self.bit(which)
            sent = lax.dynamic_index_in_dim(sums, 1 - own, axis, keepdims=False)
            kept = lax.dynamic_index_in_dim(sums, own, axis, keepdims=False)
            sums = kept + self.exchange(sent, which)
        return sums

    def gather_pair(self, values):
        got = self.gather(values, [self.core] + self.ch)
        return got.reshape((-1,) + values.shape[1:])

    def sum_pair(self, values):
        for which in [self.core] + self.ch:
            values = values + self.exchange(values.astype(BF16), which).astype(F32)
        return values


def norm_forward(values):
    average = jnp.mean(values, axis=0, keepdims=True)
    spread = jnp.mean(values * values, axis=0, keepdims=True) - average * average
    inverse = lax.rsqrt(spread + EPSILON)
    return (values - average) * inverse, inverse


def norm_backward(grad_normed, normed, inverse):
    first = jnp.mean(grad_normed, axis=0, keepdims=True)
    cross = jnp.mean(grad_normed * normed, axis=0, keepdims=True)
    return inverse * (grad_normed - first - normed * cross)


def attend_kernel(q_ref, k_ref, v_ref, out_ref, log_ref, *, block):
    length = q_ref.shape[1]
    scale = LOG2E / math.sqrt(HEAD)
    key_t = k_ref[...].T
    value = v_ref[...]
    for start in range(0, length, block):
        at = slice(start, start + block)
        scores = jnp.dot(key_t, q_ref[:, at], preferred_element_type=F32)
        top = jnp.max(scores, axis=0, keepdims=True)
        powers = jnp.exp2((scores - top) * scale)
        total = jnp.sum(powers, axis=0, keepdims=True)
        out = jnp.dot(value, powers.astype(BF16), preferred_element_type=F32)
        out_ref[:, at] = (out / total).astype(BF16)
        log_ref[0, :, at] = top * scale + jnp.log2(total)


def attend(query, key, value):
    width, length = query.shape
    head = pl.BlockSpec((HEAD, length), lambda h: (h, 0))
    return pl.pallas_call(
        functools.partial(attend_kernel, block=min(BLOCK, length)),
        grid=(width // HEAD,),
        in_specs=[head] * 3,
        out_specs=[head, pl.BlockSpec((1, 1, length), lambda h: (h, 0, 0))],
        out_shape=[
            jax.ShapeDtypeStruct((width, length), BF16),
            jax.ShapeDtypeStruct((width // HEAD, 1, length), F32),
        ],
        compiler_params=pltpu.CompilerParams(vmem_limit_bytes=VMEM_LIMIT),
        cost_estimate=pl.CostEstimate(
            flops=4 * width * length * length,
            transcendentals=width // HEAD * length * length,
            bytes_accessed=8 * width * length,
        ),
        name="attend",
    )(query, key, value)


def attend_back_kernel(q_ref, k_ref, v_ref, log_ref, a_ref, g_ref, dq_ref, dk_ref, dv_ref, s_ref, *, block):
    length = q_ref.shape[1]
    scale = LOG2E / math.sqrt(HEAD)
    unit = 1.0 / math.sqrt(HEAD)
    query_t, key_t, value_t, grad_t = [r[...].T for r in (q_ref, k_ref, v_ref, g_ref)]
    key = k_ref[...]
    delta = jnp.sum(g_ref[...].astype(F32) * a_ref[...].astype(F32), axis=0, keepdims=True)
    grad_key = jnp.zeros((length, HEAD), F32)
    grad_value = jnp.zeros((length, HEAD), F32)
    query_sum = jnp.zeros((HEAD, 1), F32)
    for start in range(0, length, block):
        at = slice(start, start + block)
        scores = jnp.dot(key_t, q_ref[:, at], preferred_element_type=F32)
        soft = jnp.exp2(scores * scale - log_ref[0, :, at])
        grad_soft = jnp.dot(value_t, g_ref[:, at], preferred_element_type=F32)
        grad_scores = (soft * (grad_soft - delta[:, at])).astype(BF16)
        grad_value += jnp.dot(soft.astype(BF16), grad_t[at], preferred_element_type=F32)
        grad_key += jnp.dot(grad_scores, query_t[at], preferred_element_type=F32)
        grad_query = jnp.dot(key, grad_scores, preferred_element_type=F32) * unit
        query_sum += jnp.sum(grad_query, axis=1, keepdims=True)
        dq_ref[:, at] = grad_query.astype(BF16)
    dk_ref[...] = (grad_key * unit).T.astype(BF16)
    grad_value = grad_value.T
    dv_ref[...] = grad_value.astype(BF16)
    s_ref[:, 0:1] = query_sum
    s_ref[:, 1:2] = jnp.sum(grad_value, axis=1, keepdims=True)


def attend_back(query, key, value, log_total, attended, grad_att):
    width, length = query.shape
    heads = width // HEAD
    head = pl.BlockSpec((HEAD, length), lambda h: (h, 0))
    log_spec = pl.BlockSpec((1, 1, length), lambda h: (h, 0, 0))
    array = jax.ShapeDtypeStruct((width, length), BF16)
    grad_query, grad_key, grad_value, sums = pl.pallas_call(
        functools.partial(attend_back_kernel, block=min(BLOCK, length)),
        grid=(heads,),
        in_specs=[head, head, head, log_spec, head, head],
        out_specs=[head, head, head, pl.BlockSpec((HEAD, 2), lambda h: (h, 0))],
        out_shape=[array, array, array, jax.ShapeDtypeStruct((width, 2), F32)],
        compiler_params=pltpu.CompilerParams(vmem_limit_bytes=VMEM_LIMIT),
        cost_estimate=pl.CostEstimate(
            flops=10 * width * length * length,
            transcendentals=heads * length * length,
            bytes_accessed=16 * width * length,
        ),
        name="attend_back",
    )(query, key, value, log_total, attended, grad_att)
    return jnp.concatenate([grad_query, grad_key, grad_value], axis=0), sums.T


def make_on_device(rows, cols):
    def on_device(
        latents,
        labels,
        timesteps,
        label_table,
        ada_weight,
        ada_bias,
        qkv_weight,
        qv_bias,
        proj_weight,
        proj_bias,
        expand_weight,
        expand_bias,
        contract_weight,
        contract_bias,
        cotangent,
    ):
        links = Links(rows, cols)
        after = lambda *v: lax.optimization_barrier(v)
        length = latents.shape[2]
        width = latents.shape[1]
        half = 3 * width // 2
        hidden_width = expand_weight.shape[1]
        hidden_half = hidden_width // 2
        seqs = labels.shape[0]
        chunk = qkv_weight.shape[0]
        row, col = lax.axis_index(ROW), lax.axis_index(COL)
        own_x, own_core = links.bit(links.x), links.bit(links.core)
        part = (col >> 1 << 1) + own_core

        gather = lambda v: lax.all_gather(v, GROUP, axis=0, tiled=True)
        qkv_own = links.swap(qkv_weight.reshape(chunk, 3 * width))
        others = [expand_weight, contract_weight.T, proj_weight.T]
        qkv_own, others = after(qkv_own, jnp.concatenate(others, axis=1))
        qkv_w = gather(qkv_own)
        others = links.swap(others)
        proj_w = links.gather_rows(others[:, 2 * hidden_width :], "a")
        others, latents_own = after(others, latents[0])
        latents_full = links.gather_pair(links.swap(latents_own))
        mlp_w = gather(others[:, : 2 * hidden_width])
        expand_w, contract_w = mlp_w[:, :hidden_width], mlp_w[:, hidden_width:]
        qkv_w, cotangent_own = after(qkv_w, cotangent[0])
        cotangent_full = links.gather_pair(links.swap(cotangent_own))
        bias_rows = [
            qv_bias.astype(F32),
            proj_bias.astype(F32)[None],
            contract_bias.astype(F32)[None],
            expand_bias.astype(F32).reshape(-1, width),
        ]
        bias_own = links.swap(jnp.concatenate(bias_rows, axis=0))
        qv_own = bias_own[:2, :, None]
        pair_bias = links.gather([bias_own[2:4]][0], [links.core] + links.ch)
        pair_bias = pair_bias.reshape(-1, 2, width).transpose(1, 0, 2).reshape(2, D, 1)
        proj_b, contract_b = pair_bias[0], pair_bias[1]
        expand_b = bias_own[4:].reshape(hidden_width, 1)

        feature = col * width + jnp.arange(width, dtype=jnp.int32)
        half_width = D // 2
        frequency = jnp.exp(-math.log(10000.0) * (feature % half_width).astype(F32) / half_width)
        angles = timesteps.astype(F32)[:, None] * frequency[None, :]
        embedding = jnp.where(feature[None, :] < half_width, jnp.cos(angles), jnp.sin(angles))
        label_hits = labels[:, None] == jnp.arange(CLASSES, dtype=jnp.int32)[None, :]
        cond_part = mm_nt(label_hits.astype(BF16), label_table) + embedding
        cond_all = links.gather(cond_part, [links.x] + links.ch)
        cond_all = cond_all.reshape(-1, seqs, width).transpose(1, 0, 2).reshape(seqs, D)
        silu_all = jax.nn.silu(cond_all).astype(BF16)
        flat_ada = ada_weight.reshape(6 * width, D)
        pair = lax.dynamic_slice_in_dim(silu_all, (row >> 1) * 2, 2, 0)
        pair_mod = mm_nt(pair, flat_ada) + ada_bias.astype(F32).reshape(1, 6 * width)
        mine = lax.dynamic_index_in_dim(pair_mod, own_x, 0)
        other = lax.dynamic_index_in_dim(pair_mod, 1 - own_x, 0)
        mod = links.joined(mine, links.exchange(other, links.x), links.x)
        mod = links.gather(mod, links.ch)
        mod = mod.reshape(-1, 6, width).transpose(1, 0, 2).reshape(6, D, 1)
        shift_first, scale_first, gate_first, shift_second, scale_second, gate_second = [
            mod[i] for i in range(6)
        ]
        own_part = lambda v: lax.dynamic_slice_in_dim(v, part * width, width, 0)

        start = latents_full.astype(F32)
        normed_first, inv_first = norm_forward(start)
        in_first = (normed_first * (1.0 + scale_first) + shift_first).astype(BF16)
        triple = mm_tn(qkv_w, in_first)
        query = (triple[:width] + qv_own[0]).astype(BF16)
        key = triple[width : 2 * width].astype(BF16)
        value = (triple[2 * width :] + qv_own[1]).astype(BF16)
        attended, log_total = attend(query, key, value)
        proj_out = links.sum_pair(mm(proj_w, attended)) + proj_b
        residual = start + gate_first * proj_out
        normed_second, inv_second = norm_forward(residual)
        in_second = (normed_second * (1.0 + scale_second) + shift_second).astype(BF16)
        pre_act = mm_tn(expand_w, in_second) + expand_b
        hidden = gelu_tanh(pre_act).astype(BF16)
        scatter = lambda v: lax.psum_scatter(v, GROUP, scatter_dimension=0, tiled=True)
        grad_out = cotangent_full.astype(F32)
        grad_mlp_b = (grad_out * gate_second).astype(BF16)
        contract_term = mm_nt(grad_mlp_b, hidden).astype(BF16)
        grad_hidden = mm_tn(contract_w, grad_mlp_b)
        grad_pre = jax.vjp(gelu_tanh, pre_act)[1](grad_hidden)[0]
        grad_pre_b = grad_pre.astype(BF16)
        expand_term = mm_nt(in_second, grad_pre_b).astype(BF16)
        grad_pre_b, expand_term = after(grad_pre_b, expand_term)
        mlp_grads = scatter(jnp.concatenate([expand_term, contract_term], axis=1))
        grad_in_second = links.sum_pair(mm(expand_w, grad_pre_b))
        grad_residual = grad_out + norm_backward(
            grad_in_second * (1.0 + scale_second), normed_second, inv_second
        )
        grad_proj_out = grad_residual * gate_first
        grad_proj_b = grad_proj_out.astype(BF16)
        proj_term = mm_nt(grad_proj_b, attended).astype(BF16)
        proj_term, grad_proj_b = after(proj_term, grad_proj_b)
        grad_proj = links.scatter_rows(proj_term, "b", rows)
        grad_att = mm_tn(proj_w, grad_proj_b).astype(BF16)
        triple_grad, qv_sums = attend_back(query, key, value, log_total, attended, grad_att)
        qkv_term = mm_nt(in_first, triple_grad).astype(BF16)
        qkv_term, triple_grad = after(qkv_term, triple_grad)
        grad_qkv = [
            links.scatter_rows(qkv_term[:, n : n + half], s, rows) for n, s in ((0, "a"), (half, "b"))
        ]
        grad_in_first = links.sum_pair(mm(qkv_w, triple_grad))
        hidden_late, _ = after(hidden, triple_grad)
        mlp_out = links.sum_pair(mm(contract_w, hidden_late)) + contract_b
        mlp_own = own_part(mlp_out)
        block_own = own_part(residual) + own_part(gate_second) * mlp_own
        block_out = links.swap(block_own.astype(BF16)).astype(F32)[None]
        grad_latents_full = grad_residual + norm_backward(
            grad_in_first * (1.0 + scale_first), normed_first, inv_first
        )
        grad_latents = links.swap(own_part(grad_latents_full).astype(BF16)).astype(F32)[None]

        token_sum = lambda v: jnp.sum(v, axis=1)[None]
        own_out = own_part(grad_out)
        own_in_second = own_part(grad_in_second)
        own_in_first = own_part(grad_in_first)
        early = jnp.concatenate(
            [
                token_sum(own_part(grad_residual) * own_part(proj_out)),
                token_sum(own_in_second),
                token_sum(own_in_second * own_part(normed_second)),
                token_sum(own_out * mlp_own),
                token_sum(own_part(grad_proj_out)),
                token_sum(own_out * own_part(gate_second)),
                jnp.sum(grad_pre, axis=1).reshape(-1, width),
            ],
            axis=0,
        )
        late = jnp.concatenate(
            [
                token_sum(own_in_first),
                token_sum(own_in_first * own_part(normed_first)),
                qv_sums,
            ],
            axis=0,
        )
        wide = lambda v: links.swap(links.gather_rows(v[None], "c"))
        early_all, late_all = wide(early), wide(late)
        grad_mod = jnp.concatenate([late_all[:, :2], early_all[:, :4]], axis=1)
        sums = jnp.sum(early_all[:, 4:], axis=0)
        grad_qv_bias = jnp.sum(late_all[:, 2:4], axis=0)
        grad_proj_bias, grad_contract_bias = sums[0], sums[1]
        grad_expand_bias = sums[2:].reshape(hidden_width)
        grad_ada_bias = jnp.sum(grad_mod, axis=0)
        flat_grad = grad_mod.reshape(seqs, 6 * width)
        grad_ada = lax.dot_general(
            flat_grad, silu_all.astype(F32), (((0,), (0,)), ((), ())), precision=HIGH
        ).reshape(6, width, D)
        grad_silu = jnp.dot(flat_grad, flat_ada.astype(F32), precision=HIGH)
        for which in [links.x] + links.ch:
            grad_silu = grad_silu + links.exchange(grad_silu, which)
        grad_cond_all = jax.vjp(jax.nn.silu, cond_all)[1](grad_silu)[0]
        grad_cond_cols = lax.dynamic_slice_in_dim(grad_cond_all, col * width, width, 1)
        grad_cond = lax.dynamic_slice_in_dim(grad_cond_cols, row, 1, 0)
        grad_table = lax.dot_general(
            grad_cond_cols, label_hits.astype(F32), (((0,), (0,)), ((), ())), precision=HIGH
        )

        grad_qkv = links.swap(jnp.concatenate(grad_qkv, axis=1)).astype(F32)
        mlp_grads = links.swap(mlp_grads)
        grad_expand = mlp_grads[:, :hidden_width].astype(F32)
        grad_contract = mlp_grads[:, hidden_width:].astype(F32).T
        return (
            block_out,
            grad_latents,
            grad_qkv.reshape(chunk, 3, width),
            grad_qv_bias,
            links.swap(grad_proj).astype(F32).T,
            grad_proj_bias,
            grad_expand,
            grad_expand_bias,
            grad_contract,
            grad_contract_bias,
            grad_ada,
            grad_ada_bias,
            grad_cond,
            grad_table,
        )

    return on_device


def solution(mesh):
    rows, cols = mesh.shape["row"], mesh.shape["col"]
    shape = (rows // 4, 2, 2, cols // 2, 2)
    fine = jax.sharding.Mesh(mesh.devices.reshape(shape), AXES)
    row, col = ROW, COL
    in_specs = (
        P(row, col, None),
        P(),
        P(),
        P(col, None),
        P(None, col, None),
        P(None, col),
        P(row, None, col),
        P(None, col),
        P(col, row),
        P(col),
        P(row, col),
        P(col),
        P(col, row),
        P(col),
        P(row, col, None),
    )
    out_specs = (
        P(row, col, None),
        P(row, col, None),
        P(row, None, col),
        P(None, col),
        P(col, row),
        P(col),
        P(row, col),
        P(col),
        P(col, row),
        P(col),
        P(None, col, None),
        P(None, col),
        P(row, col),
        P(col, None),
    )
    return jax.shard_map(
        make_on_device(rows, cols),
        mesh=fine,
        in_specs=in_specs,
        out_specs=out_specs,
        check_vma=False,
    )
```

```python
import functools
import math

import jax
import jax.numpy as jnp
from jax import lax
from jax.experimental import pallas as pl
from jax.experimental.pallas import tpu as pltpu
from jax.sharding import PartitionSpec as P

D = 1152
HEAD = 72
CLASSES = 1001
EPSILON = 1e-06
GELU_COEF = 0.7978845608028654
AXES = ("rz", "ry", "rl", "ch", "cl")
ROW, COL = AXES[:3], AXES[3:]
GROUP = ("rz", "ry", "cl")
F32 = jnp.float32
BF16 = jnp.bfloat16
HIGH = lax.Precision.HIGHEST
LOG2E = math.log2(math.e)
BLOCK = 256
VMEM_LIMIT = 48 * 1024 * 1024


def gelu_tanh(values):
    return (
        0.5 * values * (1.0 + jnp.tanh(GELU_COEF * (values + 0.044715 * values * values * values)))
    )


def mm(left, right):
    return lax.dot_general(left, right, (((1,), (0,)), ((), ())), preferred_element_type=F32)


def mm_tn(left, right):
    return lax.dot_general(left, right, (((0,), (0,)), ((), ())), preferred_element_type=F32)


def mm_nt(left, right):
    return lax.dot_general(left, right, (((1,), (1,)), ((), ())), preferred_element_type=F32)


class Links:
    def __init__(self, rows, cols):
        self.count = rows * cols
        self.col_bits = cols.bit_length() - 1
        self.row_bits = rows.bit_length() - 1
        self.flat = lax.axis_index(AXES)
        self.x = 0
        self.ch = list(range(1, self.col_bits))
        self.core = self.col_bits
        self.rh = list(range(self.core + 1, self.core + self.row_bits))[::-1]
        self.order = {
            "a": self.rh + [self.x],
            "b": self.rh[:-1] + [self.x] + self.rh[-1:],
            "c": [self.x] + self.rh[::-1],
        }

    def bit(self, which):
        return (self.flat >> which) & 1

    def exchange(self, values, which):
        pairs = [(i, i ^ (1 << which)) for i in range(self.count)]
        return lax.ppermute(values, AXES, pairs)

    def swap(self, values):
        low, high = 1, 1 << self.core
        pairs = [
            (i, i ^ (low | high))
            for i in range(self.count)
            if bool(i & low) != bool(i & high)
        ]
        moved = lax.ppermute(values, AXES, pairs)
        return jnp.where(self.bit(self.x) == self.bit(self.core), values, moved)

    def joined(self, mine, theirs, which):
        low = self.bit(which) == 0
        return jnp.where(low, jnp.stack([mine, theirs]), jnp.stack([theirs, mine]))

    def gather(self, values, order):
        for which in order:
            values = self.joined(values, self.exchange(values, which), which)
        return values

    def gather_rows(self, values, stream):
        order = self.order[stream]
        natural = self.rh + [self.x]
        got = self.gather(values, order)
        have = order[::-1]
        tail = list(range(len(have), got.ndim))
        got = got.transpose([have.index(w) for w in natural] + tail)
        return got.reshape((-1,) + values.shape[1:])

    def halves(self, sums, natural, which):
        axis = natural.index(which)
        own = self.bit(which)
        sent = lax.dynamic_index_in_dim(sums, 1 - own, axis, keepdims=False)
        kept = lax.dynamic_index_in_dim(sums, own, axis, keepdims=False)
        return kept, self.exchange(sent, which), natural[:axis] + natural[axis + 1 :]

    def split_rows(self, values, rows):
        natural = self.rh + [self.x]
        shape = (2,) * len(natural) + (values.shape[0] // rows,) + values.shape[1:]
        return values.reshape(shape), natural

    def scatter_rows(self, values, stream, rows):
        sums, natural = self.split_rows(values, rows)
        for which in self.order[stream][::-1]:
            kept, got, natural = self.halves(sums, natural, which)
            sums = kept + got
        return sums

    def gather_pair(self, values):
        got = self.gather(values, [self.core] + self.ch)
        return got.reshape((-1,) + values.shape[1:])

    def sum_pair(self, values):
        for which in [self.core] + self.ch:
            values = values + self.exchange(values.astype(BF16), which).astype(F32)
        return values


def norm_forward(values):
    average = jnp.mean(values, axis=0, keepdims=True)
    spread = jnp.mean(values * values, axis=0, keepdims=True) - average * average
    inverse = lax.rsqrt(spread + EPSILON)
    return (values - average) * inverse, inverse


def norm_backward(grad_normed, normed, inverse):
    first = jnp.mean(grad_normed, axis=0, keepdims=True)
    cross = jnp.mean(grad_normed * normed, axis=0, keepdims=True)
    return inverse * (grad_normed - first - normed * cross)


def attend_kernel(q_ref, k_ref, v_ref, out_ref, log_ref, *, block):
    length = q_ref.shape[1]
    scale = LOG2E / math.sqrt(HEAD)
    key_t = k_ref[...].T
    value = v_ref[...]
    for start in range(0, length, block):
        at = slice(start, start + block)
        scores = jnp.dot(key_t, q_ref[:, at], preferred_element_type=F32)
        top = jnp.max(scores, axis=0, keepdims=True)
        powers = jnp.exp2((scores - top) * scale)
        total = jnp.sum(powers, axis=0, keepdims=True)
        out = jnp.dot(value, powers.astype(BF16), preferred_element_type=F32)
        out_ref[:, at] = (out / total).astype(BF16)
        log_ref[0, :, at] = top * scale + jnp.log2(total)


def attend(query, key, value):
    width, length = query.shape
    head = pl.BlockSpec((HEAD, length), lambda h: (h, 0))
    return pl.pallas_call(
        functools.partial(attend_kernel, block=min(BLOCK, length)),
        grid=(width // HEAD,),
        in_specs=[head] * 3,
        out_specs=[head, pl.BlockSpec((1, 1, length), lambda h: (h, 0, 0))],
        out_shape=[
            jax.ShapeDtypeStruct((width, length), BF16),
            jax.ShapeDtypeStruct((width // HEAD, 1, length), F32),
        ],
        compiler_params=pltpu.CompilerParams(vmem_limit_bytes=VMEM_LIMIT),
        cost_estimate=pl.CostEstimate(
            flops=4 * width * length * length,
            transcendentals=width // HEAD * length * length,
            bytes_accessed=8 * width * length,
        ),
        name="attend",
    )(query, key, value)


def attend_back_kernel(q_ref, k_ref, v_ref, log_ref, a_ref, g_ref, dq_ref, dk_ref, dv_ref, s_ref, *, block):
    length = q_ref.shape[1]
    scale = LOG2E / math.sqrt(HEAD)
    unit = 1.0 / math.sqrt(HEAD)
    query_t, key_t, value_t, grad_t = [r[...].T for r in (q_ref, k_ref, v_ref, g_ref)]
    key = k_ref[...]
    delta = jnp.sum(g_ref[...].astype(F32) * a_ref[...].astype(F32), axis=0, keepdims=True)
    grad_key = jnp.zeros((length, HEAD), F32)
    grad_value = jnp.zeros((length, HEAD), F32)
    query_sum = jnp.zeros((HEAD, 1), F32)
    for start in range(0, length, block):
        at = slice(start, start + block)
        scores = jnp.dot(key_t, q_ref[:, at], preferred_element_type=F32)
        soft = jnp.exp2(scores * scale - log_ref[0, :, at])
        grad_soft = jnp.dot(value_t, g_ref[:, at], preferred_element_type=F32)
        grad_scores = (soft * (grad_soft - delta[:, at])).astype(BF16)
        grad_value += jnp.dot(soft.astype(BF16), grad_t[at], preferred_element_type=F32)
        grad_key += jnp.dot(grad_scores, query_t[at], preferred_element_type=F32)
        grad_query = jnp.dot(key, grad_scores, preferred_element_type=F32) * unit
        query_sum += jnp.sum(grad_query, axis=1, keepdims=True)
        dq_ref[:, at] = grad_query.astype(BF16)
    dk_ref[...] = (grad_key * unit).T.astype(BF16)
    grad_value = grad_value.T
    dv_ref[...] = grad_value.astype(BF16)
    s_ref[:, 0:1] = query_sum
    s_ref[:, 1:2] = jnp.sum(grad_value, axis=1, keepdims=True)


def attend_back(query, key, value, log_total, attended, grad_att):
    width, length = query.shape
    heads = width // HEAD
    head = pl.BlockSpec((HEAD, length), lambda h: (h, 0))
    log_spec = pl.BlockSpec((1, 1, length), lambda h: (h, 0, 0))
    array = jax.ShapeDtypeStruct((width, length), BF16)
    grad_query, grad_key, grad_value, sums = pl.pallas_call(
        functools.partial(attend_back_kernel, block=min(BLOCK, length)),
        grid=(heads,),
        in_specs=[head, head, head, log_spec, head, head],
        out_specs=[head, head, head, pl.BlockSpec((HEAD, 2), lambda h: (h, 0))],
        out_shape=[array, array, array, jax.ShapeDtypeStruct((width, 2), F32)],
        compiler_params=pltpu.CompilerParams(vmem_limit_bytes=VMEM_LIMIT),
        cost_estimate=pl.CostEstimate(
            flops=10 * width * length * length,
            transcendentals=heads * length * length,
            bytes_accessed=16 * width * length,
        ),
        name="attend_back",
    )(query, key, value, log_total, attended, grad_att)
    return jnp.concatenate([grad_query, grad_key, grad_value], axis=0), sums.T


def make_on_device(rows, cols):
    def on_device(
        latents,
        labels,
        timesteps,
        label_table,
        ada_weight,
        ada_bias,
        qkv_weight,
        qv_bias,
        proj_weight,
        proj_bias,
        expand_weight,
        expand_bias,
        contract_weight,
        contract_bias,
        cotangent,
    ):
        links = Links(rows, cols)
        after = lambda *v: lax.optimization_barrier(v)
        length = latents.shape[2]
        width = latents.shape[1]
        half = 3 * width // 2
        hidden_width = expand_weight.shape[1]
        hidden_half = hidden_width // 2
        seqs = labels.shape[0]
        chunk = qkv_weight.shape[0]
        row, col = lax.axis_index(ROW), lax.axis_index(COL)
        own_x, own_core = links.bit(links.x), links.bit(links.core)
        part = (col >> 1 << 1) + own_core

        gather = lambda v: lax.all_gather(v, GROUP, axis=0, tiled=True)
        qkv_own = links.swap(qkv_weight.reshape(chunk, 3 * width))
        others = [expand_weight, contract_weight.T, proj_weight.T]
        qkv_own, others = after(qkv_own, jnp.concatenate(others, axis=1))
        qkv_w = gather(qkv_own)
        others = links.swap(others)
        proj_w = links.gather_rows(others[:, 2 * hidden_width :], "a")
        others, latents_own = after(others, latents[0])
        latents_full = links.gather_pair(links.swap(latents_own))
        mlp_w = gather(others[:, : 2 * hidden_width])
        expand_w, contract_w = mlp_w[:, :hidden_width], mlp_w[:, hidden_width:]
        qkv_w, cotangent_own = after(qkv_w, cotangent[0])
        cotangent_full = links.gather_pair(links.swap(cotangent_own))
        bias_rows = [
            qv_bias.astype(F32),
            proj_bias.astype(F32)[None],
            contract_bias.astype(F32)[None],
            expand_bias.astype(F32).reshape(-1, width),
        ]
        bias_own = links.swap(jnp.concatenate(bias_rows, axis=0))
        qv_own = bias_own[:2, :, None]
        pair_bias = links.gather([bias_own[2:4]][0], [links.core] + links.ch)
        pair_bias = pair_bias.reshape(-1, 2, width).transpose(1, 0, 2).reshape(2, D, 1)
        proj_b, contract_b = pair_bias[0], pair_bias[1]
        expand_b = bias_own[4:].reshape(hidden_width, 1)

        feature = col * width + jnp.arange(width, dtype=jnp.int32)
        half_width = D // 2
        frequency = jnp.exp(-math.log(10000.0) * (feature % half_width).astype(F32) / half_width)
        angles = timesteps.astype(F32)[:, None] * frequency[None, :]
        embedding = jnp.where(feature[None, :] < half_width, jnp.cos(angles), jnp.sin(angles))
        label_hits = labels[:, None] == jnp.arange(CLASSES, dtype=jnp.int32)[None, :]
        cond_part = mm_nt(label_hits.astype(BF16), label_table) + embedding
        cond_all = links.gather(cond_part, [links.x] + links.ch)
        cond_all = cond_all.reshape(-1, seqs, width).transpose(1, 0, 2).reshape(seqs, D)
        silu_all = jax.nn.silu(cond_all).astype(BF16)
        flat_ada = ada_weight.reshape(6 * width, D)
        pair = lax.dynamic_slice_in_dim(silu_all, (row >> 1) * 2, 2, 0)
        pair_mod = mm_nt(pair, flat_ada) + ada_bias.astype(F32).reshape(1, 6 * width)
        mine = lax.dynamic_index_in_dim(pair_mod, own_x, 0)
        other = lax.dynamic_index_in_dim(pair_mod, 1 - own_x, 0)
        mod = links.joined(mine, links.exchange(other, links.x), links.x)
        mod = links.gather(mod, links.ch)
        mod = mod.reshape(-1, 6, width).transpose(1, 0, 2).reshape(6, D, 1)
        shift_first, scale_first, gate_first, shift_second, scale_second, gate_second = [
            mod[i] for i in range(6)
        ]
        own_part = lambda v: lax.dynamic_slice_in_dim(v, part * width, width, 0)

        start = latents_full.astype(F32)
        normed_first, inv_first = norm_forward(start)
        in_first = (normed_first * (1.0 + scale_first) + shift_first).astype(BF16)
        triple = mm_tn(qkv_w, in_first)
        query = (triple[:width] + qv_own[0]).astype(BF16)
        key = triple[width : 2 * width].astype(BF16)
        value = (triple[2 * width :] + qv_own[1]).astype(BF16)
        attended, log_total = attend(query, key, value)
        proj_out = links.sum_pair(mm(proj_w, attended)) + proj_b
        residual = start + gate_first * proj_out
        normed_second, inv_second = norm_forward(residual)
        in_second = (normed_second * (1.0 + scale_second) + shift_second).astype(BF16)
        pre_act = mm_tn(expand_w, in_second) + expand_b
        hidden = gelu_tanh(pre_act).astype(BF16)
        scatter = lambda v: lax.psum_scatter(v, GROUP, scatter_dimension=0, tiled=True)
        grad_out = cotangent_full.astype(F32)
        grad_mlp_b = (grad_out * gate_second).astype(BF16)
        contract_term = mm_nt(grad_mlp_b, hidden).astype(BF16)
        grad_hidden = mm_tn(contract_w, grad_mlp_b)
        grad_pre = jax.vjp(gelu_tanh, pre_act)[1](grad_hidden)[0]
        grad_pre_b = grad_pre.astype(BF16)
        expand_term = mm_nt(in_second, grad_pre_b).astype(BF16)
        grad_pre_b, expand_term = after(grad_pre_b, expand_term)
        mlp_grads = scatter(jnp.concatenate([expand_term, contract_term], axis=1))
        grad_in_second = links.sum_pair(mm(expand_w, grad_pre_b))
        grad_residual = grad_out + norm_backward(
            grad_in_second * (1.0 + scale_second), normed_second, inv_second
        )
        grad_proj_out = grad_residual * gate_first
        grad_proj_b = grad_proj_out.astype(BF16)
        proj_term = mm_nt(grad_proj_b, attended).astype(BF16)
        proj_term, grad_proj_b = after(proj_term, grad_proj_b)
        grad_proj = links.scatter_rows(proj_term, "b", rows)
        grad_att = mm_tn(proj_w, grad_proj_b).astype(BF16)
        triple_grad, qv_sums = attend_back(query, key, value, log_total, attended, grad_att)
        qkv_term = mm_nt(in_first, triple_grad).astype(BF16)
        qkv_term, triple_grad = after(qkv_term, triple_grad)
        streams = [
            (*links.split_rows(qkv_term[:, n : n + half], rows), links.order[s][::-1])
            for n, s in ((0, "a"), (half, "b"))
        ]

        def send():
            return [links.halves(sums, natural, order[0]) for sums, natural, order in streams]

        def add(sent, *others):
            done = after(*[got for _, got, _ in sent], *others)
            for i, (kept, _, natural) in enumerate(sent):
                streams[i] = (kept + done[i], natural, streams[i][2][1:])
            return done[len(sent) :]

        sent = send()
        grad_in_first = links.sum_pair(mm(qkv_w, triple_grad))
        grad_latents_full = grad_residual + norm_backward(
            grad_in_first * (1.0 + scale_first), normed_first, inv_first
        )
        grad_latents_own = own_part(grad_latents_full).astype(BF16)
        grad_in_first, grad_latents_own = add(sent, grad_in_first, grad_latents_own)
        sent = send()
        hidden_late, _ = after(hidden, triple_grad)
        mlp_out = links.sum_pair(mm(contract_w, hidden_late)) + contract_b
        mlp_own = own_part(mlp_out)
        block_own = own_part(residual) + own_part(gate_second) * mlp_own
        grad_latents_moved = links.swap(grad_latents_own)

        token_sum = lambda v: jnp.sum(v, axis=1)[None]
        own_out = own_part(grad_out)
        own_in_second = own_part(grad_in_second)
        own_in_first = own_part(grad_in_first)
        tokens = jnp.concatenate(
            [
                token_sum(own_in_first),
                token_sum(own_in_first * own_part(normed_first)),
                token_sum(own_part(grad_residual) * own_part(proj_out)),
                token_sum(own_in_second),
                token_sum(own_in_second * own_part(normed_second)),
                token_sum(own_out * mlp_own),
                qv_sums,
                token_sum(own_part(grad_proj_out)),
                token_sum(own_out * own_part(gate_second)),
                jnp.sum(grad_pre, axis=1).reshape(-1, width),
            ],
            axis=0,
        )
        tokens, grad_latents_moved = add(sent, tokens, grad_latents_moved)
        sent = send()
        grad_latents = grad_latents_moved.astype(F32)[None]
        block_moved = links.swap(block_own.astype(BF16))
        tokens_all = links.swap(links.gather_rows(tokens[None], "c"))
        tokens_all, block_moved = add(sent, tokens_all, block_moved)
        block_out = block_moved.astype(F32)[None]
        while streams[0][2]:
            add(send())
        grad_qkv = [sums for sums, _, _ in streams]
        grad_mod = tokens_all[:, :6]
        sums = jnp.sum(tokens_all[:, 6:], axis=0)
        grad_qv_bias, grad_proj_bias, grad_contract_bias = sums[:2], sums[2], sums[3]
        grad_expand_bias = sums[4:].reshape(hidden_width)
        grad_ada_bias = jnp.sum(grad_mod, axis=0)
        flat_grad = grad_mod.reshape(seqs, 6 * width)
        grad_ada = lax.dot_general(
            flat_grad, silu_all.astype(F32), (((0,), (0,)), ((), ())), precision=HIGH
        ).reshape(6, width, D)
        grad_silu = jnp.dot(flat_grad, flat_ada.astype(F32), precision=HIGH)
        for which in [links.x] + links.ch:
            grad_silu = grad_silu + links.exchange(grad_silu, which)
        grad_cond_all = jax.vjp(jax.nn.silu, cond_all)[1](grad_silu)[0]
        grad_cond_cols = lax.dynamic_slice_in_dim(grad_cond_all, col * width, width, 1)
        grad_cond = lax.dynamic_slice_in_dim(grad_cond_cols, row, 1, 0)
        grad_table = lax.dot_general(
            grad_cond_cols, label_hits.astype(F32), (((0,), (0,)), ((), ())), precision=HIGH
        )

        grad_qkv = links.swap(jnp.concatenate(grad_qkv, axis=1)).astype(F32)
        mlp_grads = links.swap(mlp_grads)
        grad_expand = mlp_grads[:, :hidden_width].astype(F32)
        grad_contract = mlp_grads[:, hidden_width:].astype(F32).T
        return (
            block_out,
            grad_latents,
            grad_qkv.reshape(chunk, 3, width),
            grad_qv_bias,
            links.swap(grad_proj).astype(F32).T,
            grad_proj_bias,
            grad_expand,
            grad_expand_bias,
            grad_contract,
            grad_contract_bias,
            grad_ada,
            grad_ada_bias,
            grad_cond,
            grad_table,
        )

    return on_device


def solution(mesh):
    rows, cols = mesh.shape["row"], mesh.shape["col"]
    shape = (rows // 4, 2, 2, cols // 2, 2)
    fine = jax.sharding.Mesh(mesh.devices.reshape(shape), AXES)
    row, col = ROW, COL
    in_specs = (
        P(row, col, None),
        P(),
        P(),
        P(col, None),
        P(None, col, None),
        P(None, col),
        P(row, None, col),
        P(None, col),
        P(col, row),
        P(col),
        P(row, col),
        P(col),
        P(col, row),
        P(col),
        P(row, col, None),
    )
    out_specs = (
        P(row, col, None),
        P(row, col, None),
        P(row, None, col),
        P(None, col),
        P(col, row),
        P(col),
        P(row, col),
        P(col),
        P(col, row),
        P(col),
        P(None, col, None),
        P(None, col),
        P(row, col),
        P(col, None),
    )
    return jax.shard_map(
        make_on_device(rows, cols),
        mesh=fine,
        in_specs=in_specs,
        out_specs=out_specs,
        check_vma=False,
    )
```
